32 devices in a mesh: groups: 2 (over x), ctx: 8 (over z, y), tp: 2 (over core).
Axes of the slice: x: 2, y: 2, z: 4, core: 2. Of those that a mesh axis runs over, the one named last changes fastest.
Arguments:
- hyena_in: bfloat16 [3, 2048, 4096], P(None, ('groups', 'ctx'), 'tp'), parts along dimension 1, may hold values from -6 to 6
- short_filter: float32 [3, 7, 4096], P(None, None, 'tp'), may hold values from -2 to 2
- mr_taps: float32 [256, 128], P('tp'), may hold values from -0.6 to 0.6
- mr_decay: float32 [256], P('tp'), may hold values from 0.005 to 0.1
- skip: float32 [4096], P('tp'), may hold values from -6 to 6
- qkv: bfloat16 [3, 2048, 2048], P(None, ('groups', 'ctx'), 'tp'), parts along dimension 1, may hold values from -8 to 8
Outputs:
- hyena_out: bfloat16 [2048, 4096], P(('groups', 'ctx'), 'tp'), parts along dimension 0
- attn_out: bfloat16 [2048, 2048], P(('groups', 'ctx'), 'tp'), parts along dimension 0
The draws below stay inside these ranges and needn't reach their ends.
There are 2 independent parts, one for each index of `groups`. The reference program is written for one: setup_inputs(seed, part) draws one part's arguments, and reference() takes and returns one part's arrays. A program takes and returns all parts, laid end to end along the dimension named above; an argument that names none is the same for every part. Nothing has to cross between parts.
All inputs are finite; a program needn't handle non-finite values.
Results may differ from the reference program's by a relative error of at most 0.008.
Values may be sent and summed in bfloat16 or wider, within the bound.
No kernel may reach another device: no remote copies, remote signals or barrier semaphores. Data moves between devices by JAX's collectives and lax.ppermute only.
A program may use at most 192 MiB of HBM per device.

```python
import math
import jax
import jax.numpy as jnp
from jax import lax

D = 4096
HEAD = 128
HEADS = 16
GW = 16
TAPS = 128
SHORT = 7
TOKENS = 1024
GROUPS = 256


def draw_qkv(key, part):
    key_base = jax.random.fold_in(key, 0)
    col_count = HEADS * HEAD
    spread = jnp.array([1.5, 1.5, 1.0], jnp.float32)[:, None, None]
    stacked = jnp.clip(jax.random.normal(key_base, (3, TOKENS, col_count), jnp.float32) * spread, -8.0, 8.0)
    return stacked.astype(jnp.bfloat16)


def block_scale(stream_key, dims, pieces, least, largest):
    level, own = 1.0, jax.random.fold_in(stream_key, 6)
    for dim, blocks in pieces:
        heights = jnp.exp(jax.random.uniform(jax.random.fold_in(own, dim), (blocks,), jnp.float32, least / len(pieces), largest / len(pieces)))
        level = level * jnp.repeat(heights, dims[dim] // blocks).reshape([-1 if axis == dim else 1 for axis in range(len(dims))])
    return level


def noise(stream_key, extent, width, bound, pieces=(), held_as=jnp.bfloat16):
    result = jax.random.normal(stream_key, extent, jnp.float32) * width
    if len(pieces) > 0:
        result = block_scale(stream_key, extent, pieces, -0.22, 0.18) * result
    return jnp.clip(result, min=-bound, max=bound).astype(held_as)


def setup_inputs(seed: int = 0, part: int = 0) -> dict:
    splits = jax.random.split(jax.random.key(seed), 7)
    own_keys = jax.random.split(jax.random.fold_in(splits[6], part), 7)
    return {
        "hyena_in": noise(own_keys[0], (3, TOKENS, D), 1.0, 6.0, ((1, 8), (2, 2))),
        "short_filter": noise(splits[1], (3, SHORT, D), SHORT ** -0.5, 2.0, ((2, 2),), jnp.float32),
        "mr_taps": noise(splits[2], (GROUPS, TAPS), 0.1, 0.6, ((0, 2),), jnp.float32),
        "mr_decay": jnp.clip(jnp.exp(math.log(0.1) - 2.9957323 * jax.random.uniform(splits[3], (GROUPS,), jnp.float32) ** block_scale(splits[3], (GROUPS,), ((0, 2),), -0.2, 0.2)), 0.005, 0.1),
        "skip": noise(splits[4], (D,), 1.0, 6.0, ((0, 2),), jnp.float32),
        "qkv": draw_qkv(jax.random.fold_in(jax.random.fold_in(splits[6], part), 71), part),
    }


def short_mix(inputs, filters_in, out_count):
    short_len = filters_in.shape[1]
    accum = jnp.zeros((inputs.shape[0], out_count, inputs.shape[2]), jnp.float32)
    for tap_index in range(short_len):
        offset = short_len - 1 - tap_index
        accum = accum + filters_in[:, tap_index][:, None, :] * inputs[:, offset:offset + out_count].astype(jnp.float32)
    return accum.astype(jnp.bfloat16)

def reference(hyena_in, short_filter, mr_taps, mr_decay, skip, qkv):
    extended = jnp.pad(hyena_in, ((0, 0), (SHORT - 1, 0), (0, 0)))
    short_out = short_mix(extended, short_filter, TOKENS)
    mixed_rows = (short_out[0].astype(jnp.float32) * short_out[2].astype(jnp.float32)).astype(jnp.bfloat16)
    filters = mr_taps * jnp.exp(-mr_decay[:, None] * jnp.arange(TAPS, dtype=jnp.float32)[None, :])
    chan_taps = jnp.repeat(filters, GW, axis=0)
    zero_padded = jnp.pad(mixed_rows.astype(jnp.float32), ((TAPS - 1, 0), (0, 0)))

    def add_tap(tap_index, accum):
        column = lax.dynamic_index_in_dim(chan_taps, tap_index, 1, keepdims=False)
        window = lax.dynamic_slice_in_dim(zero_padded, TAPS - 1 - tap_index, TOKENS, 0)
        return accum + column[None, :] * window
    conv_out = lax.fori_loop(0, TAPS, add_tap, jnp.zeros((TOKENS, D), jnp.float32))
    hyena_out = (short_out[1].astype(jnp.float32) * (conv_out + skip[None, :] * mixed_rows.astype(jnp.float32))).astype(jnp.bfloat16)
    score_scale = 1.0 / math.sqrt(HEAD)
    positions = jnp.arange(TOKENS, dtype=jnp.int32)
    causal_mask = positions[None, :] <= positions[:, None]

    def one_head(head_index):
        first_col = head_index * HEAD
        queries = lax.dynamic_slice_in_dim(qkv[0], first_col, HEAD, 1)
        keys_head = lax.dynamic_slice_in_dim(qkv[1], first_col, HEAD, 1)
        values_head = lax.dynamic_slice_in_dim(qkv[2], first_col, HEAD, 1)
        scores = jnp.dot(queries, keys_head.T, preferred_element_type=jnp.float32) * score_scale
        masked = jnp.where(causal_mask, scores, -jnp.inf)
        row_max = lax.optimization_barrier(jnp.max(masked, axis=1, keepdims=True))
        weights = jnp.where(causal_mask, jnp.exp(scores - row_max), 0.0)
        row_total = lax.optimization_barrier(jnp.sum(weights, axis=1, keepdims=True))
        summed = jnp.dot(weights.astype(jnp.bfloat16), values_head, preferred_element_type=jnp.float32)
        return summed / row_total
    per_head = lax.map(one_head, jnp.arange(HEADS, dtype=jnp.int32))
    attn_out = per_head.transpose(1, 0, 2).reshape(TOKENS, HEADS * HEAD).astype(jnp.bfloat16)
    return (hyena_out, attn_out)
```

```python
import math

import jax
import jax.numpy as jnp
from jax import lax
from jax.experimental import pallas as pl
from jax.experimental.pallas import tpu as pltpu
from jax.sharding import PartitionSpec as P

HEAD = 128
GW = 16
LANES = 128
EDGE = 8


def passed_along(block, axis, distance):
    devices = range(lax.axis_size(axis))
    route = [(i - distance, i) for i in devices if i - distance in devices]
    return lax.ppermute(block, axis, route)


def short_mix(x, edge, short_filter):
    streams, rows, width = x.shape
    taps = short_filter.shape[1]
    cols = min(512, width)

    def body(x_ref, edge_ref, filt_ref, mixed_ref, gate_ref, ext_ref):
        out = []
        for s in range(streams):
            ext_ref[s, :EDGE, :] = edge_ref[s].astype(jnp.float32)
            ext_ref[s, EDGE:, :] = x_ref[s].astype(jnp.float32)
        for c in range(cols // LANES):
            at = pl.ds(c * LANES, LANES)
            out = []
            for s in range(streams):
                accum = None
                for j in reversed(range(taps)):
                    part = filt_ref[s, j : j + 1, at] * ext_ref[s, pl.ds(EDGE - j, rows), at]
                    accum = part if accum is None else accum + part
                out.append(accum.astype(jnp.bfloat16))
            mixed_ref[:, at] = (out[0].astype(jnp.float32) * out[2].astype(jnp.float32)).astype(
                jnp.bfloat16
            )
            gate_ref[:, at] = out[1]

    return pl.pallas_call(
        body,
        name="short_mix",
        grid=(width // cols,),
        in_specs=[
            pl.BlockSpec((streams, rows, cols), lambda c: (0, 0, c)),
            pl.BlockSpec((streams, EDGE, cols), lambda c: (0, 0, c)),
            pl.BlockSpec((streams, taps, cols), lambda c: (0, 0, c)),
        ],
        out_specs=[
            pl.BlockSpec((rows, cols), lambda c: (0, c)),
            pl.BlockSpec((rows, cols), lambda c: (0, c)),
        ],
        out_shape=[jax.ShapeDtypeStruct((rows, width), jnp.bfloat16)] * 2,
        scratch_shapes=[pltpu.VMEM((streams, rows + EDGE, cols), jnp.float32)],
        cost_estimate=pl.CostEstimate(
            flops=2 * streams * taps * rows * width,
            transcendentals=0,
            bytes_accessed=10 * rows * width,
        ),
    )(x, edge, short_filter)


def long_conv(prev, mixed, gate, filters_back, skip):
    rows, width = mixed.shape
    taps = filters_back.shape[1]
    cols = min(512, width)
    per_block = LANES // GW

    def body(prev_ref, mixed_ref, gate_ref, filt_ref, skip_ref, out_ref, band_ref):
        row = lax.broadcasted_iota(jnp.int32, (rows, taps), 0)
        col = lax.broadcasted_iota(jnp.int32, (rows, taps), 1)
        lane_group = lax.broadcasted_iota(jnp.int32, (rows, LANES), 1) // GW
        for c in range(cols // LANES):
            at = pl.ds(c * LANES, LANES)
            for g in range(per_block):
                base = jnp.broadcast_to(filt_ref[pl.ds(c * per_block + g, 1), :], (rows, taps))
                ring = pltpu.roll(base, 0, 1, stride=1, stride_axis=0)
                band_ref[c, pl.ds(g * rows, rows), :taps] = jnp.where(col > row, ring, 0.0).astype(
                    jnp.bfloat16
                )
                band_ref[c, pl.ds(g * rows, rows), taps:] = jnp.where(col <= row, ring, 0.0).astype(
                    jnp.bfloat16
                )
            here = mixed_ref[:, at]
            both = jnp.concatenate([prev_ref[:, at], here], 0)
            conv_all = jnp.dot(band_ref[c], both, preferred_element_type=jnp.float32)
            conv = conv_all[:rows]
            for g in range(1, per_block):
                conv = jnp.where(lane_group == g, conv_all[g * rows : (g + 1) * rows], conv)
            out_ref[:, at] = (
                gate_ref[:, at].astype(jnp.float32)
                * (conv + skip_ref[:, at] * here.astype(jnp.float32))
            ).astype(jnp.bfloat16)

    wide = pl.BlockSpec((rows, cols), lambda c: (0, c))
    return pl.pallas_call(
        body,
        name="long_conv",
        grid=(width // cols,),
        in_specs=[
            wide,
            wide,
            wide,
            pl.BlockSpec((cols // GW, taps), lambda c: (c, 0)),
            pl.BlockSpec((1, cols), lambda c: (0, c)),
        ],
        out_specs=wide,
        out_shape=jax.ShapeDtypeStruct((rows, width), jnp.bfloat16),
        scratch_shapes=[pltpu.VMEM((cols // LANES, per_block * rows, 2 * taps), jnp.bfloat16)],
        cost_estimate=pl.CostEstimate(
            flops=2 * (width // GW) * LANES * rows * 2 * taps,
            transcendentals=0,
            bytes_accessed=10 * rows * width,
        ),
    )(prev, mixed, gate, filters_back, skip)


def head_attention(blocks, scale):
    parts, _, rows, width = blocks.shape
    step = 2 if parts % 2 == 0 else 1
    q_rows = step * rows

    def body(in_ref, out_ref):
        row = lax.broadcasted_iota(jnp.int32, (q_rows, q_rows), 0)
        col = lax.broadcasted_iota(jnp.int32, (q_rows, q_rows), 1)
        keep = col <= row
        for h in range(width // HEAD):
            at = pl.ds(h * HEAD, HEAD)
            for b in range(parts // step):
                upto = (b + 1) * step
                query = in_ref[b * step : upto, 0, :, at].reshape(q_rows, HEAD)
                keys = in_ref[:upto, 1, :, at].reshape(upto * rows, HEAD)
                values = in_ref[:upto, 2, :, at].reshape(upto * rows, HEAD)
                scores = lax.dot_general(
                    query, keys, (((1,), (1,)), ((), ())), preferred_element_type=jnp.float32
                )
                low = b * q_rows
                edge_scores = jnp.where(keep, scores[:, low:], -1e30)
                if b:
                    scores = jnp.concatenate([scores[:, :low], edge_scores], 1)
                else:
                    scores = edge_scores
                top = jnp.max(scores, axis=1, keepdims=True)
                weights = jnp.exp((scores - top) * scale)
                total = jnp.sum(weights, axis=1, keepdims=True)
                summed = jnp.dot(
                    weights.astype(jnp.bfloat16), values, preferred_element_type=jnp.float32
                )
                out_ref[b * step : upto, :, at] = (
                    (summed / total).astype(jnp.bfloat16).reshape(step, rows, HEAD)
                )

    tokens = parts * rows
    return pl.pallas_call(
        body,
        name="head_attention",
        out_shape=jax.ShapeDtypeStruct((parts, rows, width), jnp.bfloat16),
        cost_estimate=pl.CostEstimate(
            flops=2 * tokens * tokens * width,
            transcendentals=tokens * tokens * width // (2 * HEAD),
            bytes_accessed=8 * tokens * width,
        ),
    )(blocks)


def gathered_attention(qkv, scale):
    tok_rows = qkv.shape[1]
    head_count = qkv.shape[2] // HEAD
    queries = qkv[0]
    query_pos = lax.axis_index("ctx") * tok_rows + jnp.arange(tok_rows, dtype=jnp.int32)
    block_pair = lax.all_gather(qkv[1:3], "ctx", axis=1, tiled=True)
    key_pos = jnp.arange(block_pair.shape[1], dtype=jnp.int32)
    causal_mask = key_pos[None, :] <= query_pos[:, None]
    out_list = []
    for head_index in range(head_count):
        cols = slice(head_index * HEAD, (head_index + 1) * HEAD)
        scores = (
            lax.dot_general(
                queries[:, cols],
                block_pair[0][:, cols],
                (((1,), (1,)), ((), ())),
                preferred_element_type=jnp.float32,
            )
            * scale
        )
        top = jnp.max(jnp.where(causal_mask, scores, -1e30), axis=1)
        weights = jnp.where(causal_mask, jnp.exp(scores - top[:, None]), 0.0)
        total = jnp.sum(weights, axis=1)
        summed = jnp.dot(
            weights.astype(jnp.bfloat16),
            block_pair[1][:, cols],
            preferred_element_type=jnp.float32,
        )
        out_list.append((summed / total[:, None]).astype(jnp.bfloat16))
    return jnp.concatenate(out_list, 1)


def traded_attention(qkv, scale):
    parts = lax.axis_size("ctx")
    tok_rows = qkv.shape[1]
    width = qkv.shape[2] // parts
    outgoing = qkv.reshape(3, tok_rows, parts, width).transpose(2, 0, 1, 3)
    blocks = lax.all_to_all(outgoing, "ctx", 0, 0, tiled=True)
    done = head_attention(blocks, scale)
    back = lax.all_to_all(done, "ctx", 0, 0, tiled=True)
    return back.transpose(1, 0, 2).reshape(tok_rows, parts * width)


def shards(hyena_in, short_filter, mr_taps, mr_decay, skip, qkv):
    tok_rows = hyena_in.shape[1]
    tap_count = mr_taps.shape[1]
    scale = 1.0 / math.sqrt(HEAD)
    if (qkv.shape[2] // HEAD) % lax.axis_size("ctx") == 0:
        attn_out = traded_attention(qkv, scale)
    else:
        attn_out = gathered_attention(qkv, scale)
    edge = passed_along(hyena_in[:, tok_rows - EDGE :, :], "ctx", 1)
    mixed, gate = short_mix(hyena_in, edge, short_filter)
    prev = passed_along(mixed, "ctx", 1)
    tap_pos = jnp.arange(tap_count, dtype=jnp.float32)
    filters = mr_taps * jnp.exp(-mr_decay[:, None] * tap_pos[None, :])
    filters_back = jnp.concatenate([filters[:, :1], filters[:, :0:-1]], 1)
    hyena_out = long_conv(prev, mixed, gate, filters_back, skip[None, :])
    return (hyena_out, attn_out)


def solution(mesh):
    placed = (
        P(None, ("groups", "ctx"), "tp"),
        P(None, None, "tp"),
        P("tp", None),
        P("tp"),
        P("tp"),
        P(None, ("groups", "ctx"), "tp"),
    )
    return jax.shard_map(
        shards,
        mesh=mesh,
        in_specs=placed,
        out_specs=(P(("groups", "ctx"), "tp"), P(("groups", "ctx"), "tp")),
        check_vma=False,
    )
```

```python
import math

import jax
import jax.numpy as jnp
from jax import lax
from jax.experimental import pallas as pl
from jax.experimental.pallas import tpu as pltpu
from jax.sharding import PartitionSpec as P

HEAD = 128
GW = 16
LANES = 128
EDGE = 8


def passed_along(block, axis, distance):
    devices = range(lax.axis_size(axis))
    route = [(i - distance, i) for i in devices if i - distance in devices]
    return lax.ppermute(block, axis, route)


def in_vmem(array):
    return pltpu.with_memory_space_constraint(array, pltpu.VMEM)


ANYWHERE = pl.BlockSpec(memory_space=pl.ANY)


def moved(copies):
    for copy in copies:
        copy.start()
    for copy in copies:
        copy.wait()


def by_head(qkv, parts):
    streams, rows, full = qkv.shape
    width = full // parts

    def body(qkv_ref, out_ref, sems):
        moved(
            [
                pltpu.make_async_copy(
                    qkv_ref.at[:, :, pl.ds(p * width, width)], out_ref.at[p], sems.at[p]
                )
                for p in range(parts)
            ]
        )

    return pl.pallas_call(
        body,
        name="by_head",
        in_specs=[ANYWHERE],
        out_specs=pl.BlockSpec(memory_space=pltpu.VMEM),
        out_shape=pltpu.VMEM((parts, streams, rows, width), qkv.dtype),
        scratch_shapes=[pltpu.SemaphoreType.DMA((parts,))],
    )(qkv)


def by_token(blocks):
    parts, rows, width = blocks.shape

    def body(in_ref, out_ref, sems):
        moved(
            [
                pltpu.make_async_copy(
                    in_ref.at[p], out_ref.at[:, pl.ds(p * width, width)], sems.at[p]
                )
                for p in range(parts)
            ]
        )

    return pl.pallas_call(
        body,
        name="by_token",
        in_specs=[pl.BlockSpec(memory_space=pltpu.VMEM)],
        out_specs=ANYWHERE,
        out_shape=jax.ShapeDtypeStruct((rows, parts * width), blocks.dtype),
        scratch_shapes=[pltpu.SemaphoreType.DMA((parts,))],
    )(in_vmem(blocks))


def tap_sum(filt_ref, s, at, ext, rows):
    accum = None
    for j in reversed(range(filt_ref.shape[1])):
        part = filt_ref[s, j : j + 1, at] * ext[s, pl.ds(EDGE - j, rows), at]
        accum = part if accum is None else accum + part
    return accum.astype(jnp.bfloat16)


def gated(first, last):
    return (first.astype(jnp.float32) * last.astype(jnp.float32)).astype(jnp.bfloat16)


def short_mix(x, short_filter):
    streams, rows, width = x.shape
    cols = min(512, width)

    def body(x_ref, filt_ref, parcel_ref, gate_ref, ext_ref):
        for s in range(streams):
            ext_ref[s, :EDGE, :] = jnp.zeros((EDGE, cols), jnp.float32)
            ext_ref[s, EDGE:, :] = x_ref[s].astype(jnp.float32)
        for c in range(cols // LANES):
            at = pl.ds(c * LANES, LANES)
            out = [tap_sum(filt_ref, s, at, ext_ref, rows) for s in range(streams)]
            parcel_ref[:rows, at] = gated(out[0], out[2])
            gate_ref[:, at] = out[1]
        parcel_ref[:EDGE, :] = x_ref[0, :EDGE, :]
        parcel_ref[rows : rows + EDGE, :] = x_ref[2, :EDGE, :]
        for s in range(streams):
            low = rows + (1 + s) * EDGE
            parcel_ref[low : low + EDGE, :] = x_ref[s, rows - EDGE :, :]

    more = rows + (1 + streams) * EDGE
    return pl.pallas_call(
        body,
        name="short_mix",
        grid=(width // cols,),
        in_specs=[
            pl.BlockSpec((streams, rows, cols), lambda c: (0, 0, c)),
            pl.BlockSpec((streams, short_filter.shape[1], cols), lambda c: (0, 0, c)),
        ],
        out_specs=[
            pl.BlockSpec((more, cols), lambda c: (0, c)),
            pl.BlockSpec((rows, cols), lambda c: (0, c)),
        ],
        out_shape=[
            jax.ShapeDtypeStruct((more, width), jnp.bfloat16),
            jax.ShapeDtypeStruct((rows, width), jnp.bfloat16),
        ],
        scratch_shapes=[pltpu.VMEM((streams, rows + EDGE, cols), jnp.float32)],
        cost_estimate=pl.CostEstimate(
            flops=2 * streams * short_filter.shape[1] * rows * width,
            transcendentals=0,
            bytes_accessed=10 * rows * width,
        ),
    )(x, short_filter)


def long_conv(before, parcel, own, x, gate, short_filter, filters_back, skip):
    streams, rows, width = x.shape
    taps = filters_back.shape[1]
    cols = min(512, width)
    per_block = LANES // GW
    more = own.shape[0]

    def body(
        before_ref,
        parcel_ref,
        own_ref,
        x_ref,
        gate_ref,
        short_ref,
        filt_ref,
        skip_ref,
        out_ref,
        band_ref,
        ext_ref,
        both_ref,
    ):
        row = lax.broadcasted_iota(jnp.int32, (rows, taps), 0)
        col = lax.broadcasted_iota(jnp.int32, (rows, taps), 1)
        lane_group = lax.broadcasted_iota(jnp.int32, (rows, LANES), 1) // GW
        starts = {0: 0, 2: rows}
        for s in range(streams):
            low = rows + (1 + s) * EDGE
            ext_ref[s, :EDGE, :] = parcel_ref[low : low + EDGE, :].astype(jnp.float32)
            ext_ref[s, EDGE:, :] = x_ref[s].astype(jnp.float32)
        for k, s in enumerate(starts):
            low = starts[s]
            ext_ref[streams + s, :EDGE, :] = before_ref[k].astype(jnp.float32)
            ext_ref[streams + s, EDGE:, :] = parcel_ref[low : low + EDGE, :].astype(jnp.float32)
        both_ref[:rows, :] = parcel_ref[:rows, :]
        both_ref[rows:, :] = own_ref[:rows, :]
        for c in range(cols // LANES):
            at = pl.ds(c * LANES, LANES)
            head = []
            for base in (0, streams):
                ends = [
                    tap_sum(short_ref, s, at, ext_ref.at[pl.ds(base, streams)], EDGE)
                    for s in starts
                ]
                head.append(gated(*ends))
            both_ref[:EDGE, at] = head[1]
            both_ref[rows : rows + EDGE, at] = head[0]
            gate_head = tap_sum(short_ref, 1, at, ext_ref, EDGE)
            for g in range(per_block):
                base = jnp.broadcast_to(filt_ref[pl.ds(c * per_block + g, 1), :], (rows, taps))
                ring = pltpu.roll(base, 0, 1, stride=1, stride_axis=0)
                band_ref[c, pl.ds(g * rows, rows), :taps] = jnp.where(col > row, ring, 0.0).astype(
                    jnp.bfloat16
                )
                band_ref[c, pl.ds(g * rows, rows), taps:] = jnp.where(col <= row, ring, 0.0).astype(
                    jnp.bfloat16
                )
            conv_all = jnp.dot(band_ref[c], both_ref[:, at], preferred_element_type=jnp.float32)
            conv = conv_all[:rows]
            for g in range(1, per_block):
                conv = jnp.where(lane_group == g, conv_all[g * rows : (g + 1) * rows], conv)
            here = both_ref[rows:, at].astype(jnp.float32)
            inner = conv + skip_ref[:, at] * here
            out_ref[:, at] = (gate_ref[:, at].astype(jnp.float32) * inner).astype(jnp.bfloat16)
            out_ref[:EDGE, at] = (gate_head.astype(jnp.float32) * inner[:EDGE]).astype(jnp.bfloat16)

    return pl.pallas_call(
        body,
        name="long_conv",
        grid=(width // cols,),
        in_specs=[
            pl.BlockSpec((2, EDGE, cols), lambda c: (0, 0, c)),
            pl.BlockSpec((more, cols), lambda c: (0, c)),
            pl.BlockSpec((more, cols), lambda c: (0, c)),
            pl.BlockSpec((streams, EDGE, cols), lambda c: (0, 0, c)),
            pl.BlockSpec((rows, cols), lambda c: (0, c)),
            pl.BlockSpec((streams, short_filter.shape[1], cols), lambda c: (0, 0, c)),
            pl.BlockSpec((cols // GW, taps), lambda c: (c, 0)),
            pl.BlockSpec((1, cols), lambda c: (0, c)),
        ],
        out_specs=pl.BlockSpec((rows, cols), lambda c: (0, c)),
        out_shape=jax.ShapeDtypeStruct((rows, width), jnp.bfloat16),
        scratch_shapes=[
            pltpu.VMEM((cols // LANES, per_block * rows, 2 * taps), jnp.bfloat16),
            pltpu.VMEM((2 * streams, 2 * EDGE, cols), jnp.float32),
            pltpu.VMEM((2 * rows, cols), jnp.bfloat16),
        ],
        cost_estimate=pl.CostEstimate(
            flops=2 * (width // GW) * LANES * rows * 2 * taps,
            transcendentals=0,
            bytes_accessed=10 * rows * width,
        ),
    )(before, parcel, own, x, gate, short_filter, filters_back, skip)


def head_attention(blocks, scale):
    parts, _, rows, width = blocks.shape
    step = 2 if parts % 2 == 0 else 1
    q_rows = step * rows

    def body(in_ref, out_ref):
        row = lax.broadcasted_iota(jnp.int32, (q_rows, q_rows), 0)
        col = lax.broadcasted_iota(jnp.int32, (q_rows, q_rows), 1)
        keep = col <= row
        for h in range(width // HEAD):
            at = pl.ds(h * HEAD, HEAD)
            for b in range(parts // step):
                upto = (b + 1) * step
                query = in_ref[b * step : upto, 0, :, at].reshape(q_rows, HEAD)
                keys = in_ref[:upto, 1, :, at].reshape(upto * rows, HEAD)
                values = in_ref[:upto, 2, :, at].reshape(upto * rows, HEAD)
                scores = lax.dot_general(
                    query, keys, (((1,), (1,)), ((), ())), preferred_element_type=jnp.float32
                )
                low = b * q_rows
                edge_scores = jnp.where(keep, scores[:, low:], -1e30)
                if b:
                    scores = jnp.concatenate([scores[:, :low], edge_scores], 1)
                else:
                    scores = edge_scores
                top = jnp.max(scores, axis=1, keepdims=True)
                weights = jnp.exp((scores - top) * scale)
                total = jnp.sum(weights, axis=1, keepdims=True)
                summed = jnp.dot(
                    weights.astype(jnp.bfloat16), values, preferred_element_type=jnp.float32
                )
                out_ref[b * step : upto, :, at] = (
                    (summed / total).astype(jnp.bfloat16).reshape(step, rows, HEAD)
                )

    tokens = parts * rows
    return pl.pallas_call(
        body,
        name="head_attention",
        in_specs=[pl.BlockSpec(memory_space=pltpu.VMEM)],
        out_specs=pl.BlockSpec(memory_space=pltpu.VMEM),
        out_shape=jax.ShapeDtypeStruct((parts, rows, width), jnp.bfloat16),
        cost_estimate=pl.CostEstimate(
            flops=2 * tokens * tokens * width,
            transcendentals=tokens * tokens * width // (2 * HEAD),
            bytes_accessed=8 * tokens * width,
        ),
    )(in_vmem(blocks))


def gathered_attention(qkv, scale):
    tok_rows = qkv.shape[1]
    head_count = qkv.shape[2] // HEAD
    queries = qkv[0]
    query_pos = lax.axis_index("ctx") * tok_rows + jnp.arange(tok_rows, dtype=jnp.int32)
    block_pair = lax.all_gather(qkv[1:3], "ctx", axis=1, tiled=True)
    key_pos = jnp.arange(block_pair.shape[1], dtype=jnp.int32)
    causal_mask = key_pos[None, :] <= query_pos[:, None]
    out_list = []
    for head_index in range(head_count):
        cols = slice(head_index * HEAD, (head_index + 1) * HEAD)
        scores = (
            lax.dot_general(
                queries[:, cols],
                block_pair[0][:, cols],
                (((1,), (1,)), ((), ())),
                preferred_element_type=jnp.float32,
            )
            * scale
        )
        top = jnp.max(jnp.where(causal_mask, scores, -1e30), axis=1)
        weights = jnp.where(causal_mask, jnp.exp(scores - top[:, None]), 0.0)
        total = jnp.sum(weights, axis=1)
        summed = jnp.dot(
            weights.astype(jnp.bfloat16),
            block_pair[1][:, cols],
            preferred_element_type=jnp.float32,
        )
        out_list.append((summed / total[:, None]).astype(jnp.bfloat16))
    return jnp.concatenate(out_list, 1)


def traded_attention(qkv, scale, early):
    parts = lax.axis_size("ctx")
    blocks = lax.all_to_all(in_vmem(by_head(qkv, parts)), "ctx", 0, 0, tiled=True)
    blocks, early = lax.optimization_barrier((blocks, early))
    done = head_attention(blocks, scale)
    return by_token(lax.all_to_all(done, "ctx", 0, 0, tiled=True)), early


def shards(hyena_in, short_filter, mr_taps, mr_decay, skip, qkv):
    tok_rows = hyena_in.shape[1]
    tap_count = mr_taps.shape[1]
    scale = 1.0 / math.sqrt(HEAD)
    before = passed_along(hyena_in[::2, tok_rows - EDGE :, :], "ctx", 2)
    own, gate = short_mix(hyena_in, short_filter)
    parcel = passed_along(own, "ctx", 1)
    tap_pos = jnp.arange(tap_count, dtype=jnp.float32)
    filters = mr_taps * jnp.exp(-mr_decay[:, None] * tap_pos[None, :])
    filters_back = jnp.concatenate([filters[:, :1], filters[:, :0:-1]], 1)
    if (qkv.shape[2] // HEAD) % lax.axis_size("ctx") == 0:
        attn_out, (before, filters_back) = traded_attention(qkv, scale, (before, filters_back))
    else:
        attn_out = gathered_attention(qkv, scale)
    hyena_out = long_conv(
        before, parcel, own, hyena_in, gate, short_filter, filters_back, skip[None, :]
    )
    return (hyena_out, attn_out)


def solution(mesh):
    placed = (
        P(None, ("groups", "ctx"), "tp"),
        P(None, None, "tp"),
        P("tp", None),
        P("tp"),
        P("tp"),
        P(None, ("groups", "ctx"), "tp"),
    )
    return jax.shard_map(
        shards,
        mesh=mesh,
        in_specs=placed,
        out_specs=(P(("groups", "ctx"), "tp"), P(("groups", "ctx"), "tp")),
        check_vma=False,
    )
```

```python
import math

import jax
import jax.numpy as jnp
from jax import lax
from jax.experimental import pallas as pl
from jax.experimental.pallas import tpu as pltpu
from jax.sharding import PartitionSpec as P

HEAD = 128
GW = 16
LANES = 128
EDGE = 8


def passed_along(block, axis, distance):
    devices = range(lax.axis_size(axis))
    route = [(i - distance, i) for i in devices if i - distance in devices]
    return lax.ppermute(block, axis, route)


def in_vmem(array):
    return pltpu.with_memory_space_constraint(array, pltpu.VMEM)


ANYWHERE = pl.BlockSpec(memory_space=pl.ANY)


def moved(copies):
    for copy in copies:
        copy.start()
    for copy in copies:
        copy.wait()


def by_head(qkv, parts):
    streams, rows, full = qkv.shape
    width = full // parts

    def body(qkv_ref, out_ref):
        for p in range(parts):
            out_ref[p] = qkv_ref[:, :, pl.ds(p * width, width)]

    return pl.pallas_call(
        body,
        name="by_head",
        in_specs=[pl.BlockSpec(memory_space=pltpu.VMEM)],
        out_specs=pl.BlockSpec(memory_space=pltpu.VMEM),
        out_shape=pltpu.VMEM((parts, streams, rows, width), qkv.dtype),
    )(in_vmem(qkv))


def by_token(blocks):
    parts, rows, width = blocks.shape

    def body(in_ref, out_ref, sems):
        moved(
            [
                pltpu.make_async_copy(
                    in_ref.at[p], out_ref.at[:, pl.ds(p * width, width)], sems.at[p]
                )
                for p in range(parts)
            ]
        )

    return pl.pallas_call(
        body,
        name="by_token",
        in_specs=[pl.BlockSpec(memory_space=pltpu.VMEM)],
        out_specs=ANYWHERE,
        out_shape=jax.ShapeDtypeStruct((rows, parts * width), blocks.dtype),
        scratch_shapes=[pltpu.SemaphoreType.DMA((parts,))],
    )(in_vmem(blocks))


def hyena_local(x, edge, short_filter, filters_back, skip):
    streams, rows, width = x.shape
    short_taps = short_filter.shape[1]
    taps = filters_back.shape[1]
    cols = min(512, width)
    per_block = LANES // GW

    def body(x_ref, edge_ref, short_ref, filt_ref, skip_ref, onward_ref, part_ref, gate_ref, *held):
        ext_ref, band_ref, twice_ref = held
        row = lax.broadcasted_iota(jnp.int32, (rows, taps), 0)
        col = lax.broadcasted_iota(jnp.int32, (rows, taps), 1)
        lane_group = (lax.broadcasted_iota(jnp.int32, (rows, 2 * LANES), 1) % LANES) // GW
        twice_ref[:rows, LANES:] = jnp.zeros((rows, LANES), jnp.bfloat16)
        twice_ref[rows:, :LANES] = jnp.zeros((rows, LANES), jnp.bfloat16)
        for s in range(streams):
            ext_ref[s, :EDGE, :] = edge_ref[s].astype(jnp.float32)
            ext_ref[s, EDGE:, :] = x_ref[s].astype(jnp.float32)
        for c in range(cols // LANES):
            at = pl.ds(c * LANES, LANES)
            out = []
            for s in range(streams):
                accum = None
                for j in reversed(range(short_taps)):
                    piece = short_ref[s, j : j + 1, at] * ext_ref[s, pl.ds(EDGE - j, rows), at]
                    accum = piece if accum is None else accum + piece
                out.append(accum.astype(jnp.bfloat16))
            mixed = (out[0].astype(jnp.float32) * out[2].astype(jnp.float32)).astype(jnp.bfloat16)
            gate_ref[:, at] = out[1]
            twice_ref[:rows, :LANES] = mixed
            twice_ref[rows:, LANES:] = mixed
            for g in range(per_block):
                base = jnp.broadcast_to(filt_ref[pl.ds(c * per_block + g, 1), :], (rows, taps))
                ring = pltpu.roll(base, 0, 1, stride=1, stride_axis=0)
                at_g = pl.ds(g * rows, rows)
                band_ref[at_g, :taps] = jnp.where(col > row, ring, 0.0).astype(jnp.bfloat16)
                band_ref[at_g, taps:] = jnp.where(col <= row, ring, 0.0).astype(jnp.bfloat16)
            every = jnp.dot(band_ref[...], twice_ref[...], preferred_element_type=jnp.float32)
            conv = every[:rows]
            for g in range(1, per_block):
                conv = jnp.where(lane_group == g, every[g * rows : (g + 1) * rows], conv)
            onward_ref[:, at] = conv[:, :LANES].astype(jnp.bfloat16)
            part_ref[:, at] = conv[:, LANES:] + skip_ref[:, at] * mixed.astype(jnp.float32)

    wide = pl.BlockSpec((rows, cols), lambda c: (0, c))
    return pl.pallas_call(
        body,
        name="hyena_local",
        grid=(width // cols,),
        in_specs=[
            pl.BlockSpec((streams, rows, cols), lambda c: (0, 0, c)),
            pl.BlockSpec((streams, EDGE, cols), lambda c: (0, 0, c)),
            pl.BlockSpec((streams, short_taps, cols), lambda c: (0, 0, c)),
            pl.BlockSpec((cols // GW, taps), lambda c: (c, 0)),
            pl.BlockSpec((1, cols), lambda c: (0, c)),
        ],
        out_specs=[wide, wide, wide],
        out_shape=[
            jax.ShapeDtypeStruct((rows, width), jnp.bfloat16),
            jax.ShapeDtypeStruct((rows, width), jnp.float32),
            jax.ShapeDtypeStruct((rows, width), jnp.bfloat16),
        ],
        scratch_shapes=[
            pltpu.VMEM((streams, rows + EDGE, cols), jnp.float32),
            pltpu.VMEM((per_block * rows, 2 * taps), jnp.bfloat16),
            pltpu.VMEM((2 * rows, 2 * LANES), jnp.bfloat16),
        ],
        cost_estimate=pl.CostEstimate(
            flops=4 * (width // GW) * LANES * rows * 2 * taps,
            transcendentals=0,
            bytes_accessed=14 * rows * width,
        ),
    )(x, edge, short_filter, filters_back, skip)


def head_attention(blocks, scale):
    parts, _, rows, width = blocks.shape
    step = 2 if parts % 2 == 0 else 1
    q_rows = step * rows

    def body(in_ref, out_ref):
        row = lax.broadcasted_iota(jnp.int32, (q_rows, q_rows), 0)
        col = lax.broadcasted_iota(jnp.int32, (q_rows, q_rows), 1)
        keep = col <= row
        for h in range(width // HEAD):
            at = pl.ds(h * HEAD, HEAD)
            for b in range(parts // step):
                upto = (b + 1) * step
                query = in_ref[b * step : upto, 0, :, at].reshape(q_rows, HEAD)
                keys = in_ref[:upto, 1, :, at].reshape(upto * rows, HEAD)
                values = in_ref[:upto, 2, :, at].reshape(upto * rows, HEAD)
                scores = lax.dot_general(
                    query, keys, (((1,), (1,)), ((), ())), preferred_element_type=jnp.float32
                )
                low = b * q_rows
                edge_scores = jnp.where(keep, scores[:, low:], -1e30)
                if b:
                    scores = jnp.concatenate([scores[:, :low], edge_scores], 1)
                else:
                    scores = edge_scores
                top = jnp.max(scores, axis=1, keepdims=True)
                weights = jnp.exp((scores - top) * scale)
                total = jnp.sum(weights, axis=1, keepdims=True)
                summed = jnp.dot(
                    weights.astype(jnp.bfloat16), values, preferred_element_type=jnp.float32
                )
                out_ref[b * step : upto, :, at] = (
                    (summed / total).astype(jnp.bfloat16).reshape(step, rows, HEAD)
                )

    tokens = parts * rows
    return pl.pallas_call(
        body,
        name="head_attention",
        in_specs=[pl.BlockSpec(memory_space=pltpu.VMEM)],
        out_specs=pl.BlockSpec(memory_space=pltpu.VMEM),
        out_shape=jax.ShapeDtypeStruct((parts, rows, width), jnp.bfloat16),
        cost_estimate=pl.CostEstimate(
            flops=2 * tokens * tokens * width,
            transcendentals=tokens * tokens * width // (2 * HEAD),
            bytes_accessed=8 * tokens * width,
        ),
    )(in_vmem(blocks))


def gathered_attention(qkv, scale):
    tok_rows = qkv.shape[1]
    head_count = qkv.shape[2] // HEAD
    queries = qkv[0]
    query_pos = lax.axis_index("ctx") * tok_rows + jnp.arange(tok_rows, dtype=jnp.int32)
    block_pair = lax.all_gather(qkv[1:3], "ctx", axis=1, tiled=True)
    key_pos = jnp.arange(block_pair.shape[1], dtype=jnp.int32)
    causal_mask = key_pos[None, :] <= query_pos[:, None]
    out_list = []
    for head_index in range(head_count):
        cols = slice(head_index * HEAD, (head_index + 1) * HEAD)
        scores = (
            lax.dot_general(
                queries[:, cols],
                block_pair[0][:, cols],
                (((1,), (1,)), ((), ())),
                preferred_element_type=jnp.float32,
            )
            * scale
        )
        top = jnp.max(jnp.where(causal_mask, scores, -1e30), axis=1)
        weights = jnp.where(causal_mask, jnp.exp(scores - top[:, None]), 0.0)
        total = jnp.sum(weights, axis=1)
        summed = jnp.dot(
            weights.astype(jnp.bfloat16),
            block_pair[1][:, cols],
            preferred_element_type=jnp.float32,
        )
        out_list.append((summed / total[:, None]).astype(jnp.bfloat16))
    return jnp.concatenate(out_list, 1)


def shards(hyena_in, short_filter, mr_taps, mr_decay, skip, qkv):
    tok_rows = hyena_in.shape[1]
    tap_count = mr_taps.shape[1]
    parts = lax.axis_size("ctx")
    scale = 1.0 / math.sqrt(HEAD)
    traded = (qkv.shape[2] // HEAD) % parts == 0
    edge = passed_along(hyena_in[:, tok_rows - EDGE :, :], "ctx", 1)
    if traded:
        outgoing, edge = lax.optimization_barrier((by_head(qkv, parts), edge))
        blocks = lax.all_to_all(outgoing, "ctx", 0, 0, tiled=True)
    tap_pos = jnp.arange(tap_count, dtype=jnp.float32)
    filters = mr_taps * jnp.exp(-mr_decay[:, None] * tap_pos[None, :])
    filters_back = jnp.concatenate([filters[:, :1], filters[:, :0:-1]], 1)
    onward, part, gate = hyena_local(hyena_in, edge, short_filter, filters_back, skip[None, :])
    carried = passed_along(onward, "ctx", 1)
    if traded:
        done = head_attention(blocks, scale)
        attn_out = by_token(lax.all_to_all(done, "ctx", 0, 0, tiled=True))
    else:
        attn_out = gathered_attention(qkv, scale)
    hyena_out = (gate.astype(jnp.float32) * (part + carried.astype(jnp.float32))).astype(
        jnp.bfloat16
    )
    return (hyena_out, attn_out)


def solution(mesh):
    placed = (
        P(None, ("groups", "ctx"), "tp"),
        P(None, None, "tp"),
        P("tp", None),
        P("tp"),
        P("tp"),
        P(None, ("groups", "ctx"), "tp"),
    )
    return jax.shard_map(
        shards,
        mesh=mesh,
        in_specs=placed,
        out_specs=(P(("groups", "ctx"), "tp"), P(("groups", "ctx"), "tp")),
        check_vma=False,
    )
```

```python
import math

import jax
import jax.numpy as jnp
from jax import lax
from jax.experimental import pallas as pl
from jax.experimental.pallas import tpu as pltpu
from jax.sharding import PartitionSpec as P

HEAD = 128
GW = 16
LANES = 128
EDGE = 8
REACH = 16


def passed_along(block, axis, distance):
    devices = range(lax.axis_size(axis))
    route = [(i - distance, i) for i in devices if i - distance in devices]
    return lax.ppermute(block, axis, route)


def in_vmem(array):
    return pltpu.with_memory_space_constraint(array, pltpu.VMEM)


ANYWHERE = pl.BlockSpec(memory_space=pl.ANY)


def moved(copies):
    for copy in copies:
        copy.start()
    for copy in copies:
        copy.wait()


def by_head(qkv, parts):
    streams, rows, full = qkv.shape
    width = full // parts

    def body(qkv_ref, out_ref):
        for p in range(parts):
            out_ref[p] = qkv_ref[:, :, pl.ds(p * width, width)]

    return pl.pallas_call(
        body,
        name="by_head",
        in_specs=[pl.BlockSpec(memory_space=pltpu.VMEM)],
        out_specs=pl.BlockSpec(memory_space=pltpu.VMEM),
        out_shape=pltpu.VMEM((parts, streams, rows, width), qkv.dtype),
    )(in_vmem(qkv))


def last_rows(x):
    streams, rows, width = x.shape
    tall = REACH + EDGE
    pieces = ((0, tall), (2, tall), (1, EDGE))

    def body(x_ref, out_ref, sems):
        copies = []
        low = 0
        for k, (s, count) in enumerate(pieces):
            copies.append(
                pltpu.make_async_copy(
                    x_ref.at[s, pl.ds(rows - count, count)],
                    out_ref.at[pl.ds(low, count)],
                    sems.at[k],
                )
            )
            low += count
        moved(copies)

    return pl.pallas_call(
        body,
        name="last_rows",
        in_specs=[ANYWHERE],
        out_specs=pl.BlockSpec(memory_space=pltpu.VMEM),
        out_shape=pltpu.VMEM((2 * tall + EDGE, width), x.dtype),
        scratch_shapes=[pltpu.SemaphoreType.DMA((len(pieces),))],
    )(x)


def by_token(blocks):
    parts, rows, width = blocks.shape

    def body(in_ref, out_ref, sems):
        moved(
            [
                pltpu.make_async_copy(
                    in_ref.at[p], out_ref.at[:, pl.ds(p * width, width)], sems.at[p]
                )
                for p in range(parts)
            ]
        )

    return pl.pallas_call(
        body,
        name="by_token",
        in_specs=[pl.BlockSpec(memory_space=pltpu.VMEM)],
        out_specs=ANYWHERE,
        out_shape=jax.ShapeDtypeStruct((rows, parts * width), blocks.dtype),
        scratch_shapes=[pltpu.SemaphoreType.DMA((parts,))],
    )(in_vmem(blocks))


def hyena_local(x, tail, short_filter, filters_back, skip):
    streams, rows, width = x.shape
    short_taps = short_filter.shape[1]
    taps = filters_back.shape[1]
    cols = min(512, width)
    per_block = LANES // GW
    tall = REACH + EDGE
    kept = rows - REACH

    def body(x_ref, tail_ref, short_ref, filt_ref, skip_ref, onward_ref, part_ref, gate_ref, *held):
        ext_ref, twice_ref, spread_ref = held
        row = lax.broadcasted_iota(jnp.int32, (rows, taps), 0)
        col = lax.broadcasted_iota(jnp.int32, (rows, taps), 1)
        lane_group = (lax.broadcasted_iota(jnp.int32, (rows, 2 * LANES), 1) % LANES) // GW
        twice_ref[:kept, LANES:] = jnp.zeros((kept, LANES), jnp.bfloat16)
        twice_ref[kept:, :LANES] = jnp.zeros((2 * rows - kept, LANES), jnp.bfloat16)
        for c in range(cols // LANES):
            at = pl.ds(c * LANES, LANES)
            ext_ref[0, c, :tall, :] = tail_ref[:tall, at].astype(jnp.float32)
            ext_ref[2, c, :tall, :] = tail_ref[tall : 2 * tall, at].astype(jnp.float32)
            ext_ref[1, c, REACH:tall, :] = tail_ref[2 * tall :, at].astype(jnp.float32)
            for s in range(streams):
                ext_ref[s, c, tall:, :] = x_ref[s, :, at].astype(jnp.float32)
            out = []
            for s, count in enumerate((REACH + rows, rows, REACH + rows)):
                low = tall + rows - count
                every = count // EDGE
                slabs = [
                    ext_ref[s, c, pl.ds(low + k, EDGE, stride=every), :]
                    for k in range(1 - short_taps, every)
                ]
                heights = [
                    jnp.broadcast_to(short_ref[s, j : j + 1, at], (EDGE, LANES))
                    for j in range(short_taps)
                ]
                sums = []
                for k in range(every):
                    accum = None
                    for j in range(short_taps):
                        piece = heights[j] * slabs[k + short_taps - 1 - j]
                        accum = piece if accum is None else accum + piece
                    sums.append(accum.astype(jnp.bfloat16).astype(jnp.float32))
                out.append(sums)
            for k, (first, last) in enumerate(zip(out[0], out[2])):
                spread_ref[0, c, pl.ds(k, EDGE, stride=len(out[0])), :] = first * last
            for k, middle in enumerate(out[1]):
                spread_ref[1, c, pl.ds(k, EDGE, stride=len(out[1])), :] = middle
            mixed = spread_ref[0, c].astype(jnp.bfloat16)
            gate_ref[:, at] = spread_ref[1, c, :rows].astype(jnp.bfloat16)
            twice_ref[:kept, :LANES] = mixed[REACH : REACH + kept]
            twice_ref[kept:, LANES:] = mixed
            conv = None
            for g in range(per_block):
                base = jnp.broadcast_to(filt_ref[pl.ds(c * per_block + g, 1), :], (rows, taps))
                ring = pltpu.roll(base, 0, 1, stride=1, stride_axis=0)
                band = jnp.concatenate([jnp.where(col > row, ring, 0.0), jnp.where(col <= row, ring, 0.0)], 1).astype(jnp.bfloat16)
                one = jnp.dot(band, twice_ref[...], preferred_element_type=jnp.float32)
                conv = one if g == 0 else jnp.where(lane_group == g, one, conv)
            onward_ref[:, at] = conv[:kept, :LANES].astype(jnp.bfloat16)
            part_ref[:, at] = conv[:, LANES:] + skip_ref[:, at] * mixed[REACH:].astype(jnp.float32)

    wide = pl.BlockSpec((rows, cols), lambda c: (0, c))
    return pl.pallas_call(
        body,
        name="hyena_local",
        grid=(width // cols,),
        in_specs=[
            pl.BlockSpec((streams, rows, cols), lambda c: (0, 0, c)),
            pl.BlockSpec((2 * tall + EDGE, cols), lambda c: (0, c)),
            pl.BlockSpec((streams, short_taps, cols), lambda c: (0, 0, c)),
            pl.BlockSpec((cols // GW, taps), lambda c: (c, 0)),
            pl.BlockSpec((1, cols), lambda c: (0, c)),
        ],
        out_specs=[pl.BlockSpec((kept, cols), lambda c: (0, c)), wide, wide],
        out_shape=[
            jax.ShapeDtypeStruct((kept, width), jnp.bfloat16),
            jax.ShapeDtypeStruct((rows, width), jnp.float32),
            jax.ShapeDtypeStruct((rows, width), jnp.bfloat16),
        ],
        scratch_shapes=[
            pltpu.VMEM((streams, cols // LANES, rows + tall, LANES), jnp.float32),
            pltpu.VMEM((2 * rows, 2 * LANES), jnp.bfloat16),
            pltpu.VMEM((2, cols // LANES, rows + REACH, LANES), jnp.float32),
        ],
        cost_estimate=pl.CostEstimate(
            flops=20 * (width // GW) * LANES * rows * 2 * taps,
            transcendentals=0,
            bytes_accessed=14 * rows * width,
        ),
    )(x, tail, short_filter, filters_back, skip)


def head_attention(blocks, scale):
    parts, _, rows, width = blocks.shape
    step = 2 if parts % 2 == 0 else 1
    q_rows = step * rows

    def body(in_ref, out_ref):
        row = lax.broadcasted_iota(jnp.int32, (q_rows, q_rows), 0)
        col = lax.broadcasted_iota(jnp.int32, (q_rows, q_rows), 1)
        keep = col <= row
        for h in range(width // HEAD):
            at = pl.ds(h * HEAD, HEAD)
            for b in range(parts // step):
                upto = (b + 1) * step
                query = in_ref[b * step : upto, 0, :, at].reshape(q_rows, HEAD)
                keys = in_ref[:upto, 1, :, at].reshape(upto * rows, HEAD)
                values = in_ref[:upto, 2, :, at].reshape(upto * rows, HEAD)
                scores = lax.dot_general(
                    query, keys, (((1,), (1,)), ((), ())), preferred_element_type=jnp.float32
                )
                low = b * q_rows
                edge_scores = jnp.where(keep, scores[:, low:], -1e30)
                if b:
                    scores = jnp.concatenate([scores[:, :low], edge_scores], 1)
                else:
                    scores = edge_scores
                top = jnp.max(scores, axis=1, keepdims=True)
                weights = jnp.exp((scores - top) * scale)
                total = jnp.sum(weights, axis=1, keepdims=True)
                summed = jnp.dot(
                    weights.astype(jnp.bfloat16), values, preferred_element_type=jnp.float32
                )
                out_ref[b * step : upto, :, at] = (
                    (summed / total).astype(jnp.bfloat16).reshape(step, rows, HEAD)
                )

    tokens = parts * rows
    return pl.pallas_call(
        body,
        name="head_attention",
        in_specs=[pl.BlockSpec(memory_space=pltpu.VMEM)],
        out_specs=pl.BlockSpec(memory_space=pltpu.VMEM),
        out_shape=jax.ShapeDtypeStruct((parts, rows, width), jnp.bfloat16),
        cost_estimate=pl.CostEstimate(
            flops=2 * tokens * tokens * width,
            transcendentals=tokens * tokens * width // (2 * HEAD),
            bytes_accessed=8 * tokens * width,
        ),
    )(in_vmem(blocks))


def gathered_attention(qkv, scale):
    tok_rows = qkv.shape[1]
    head_count = qkv.shape[2] // HEAD
    queries = qkv[0]
    query_pos = lax.axis_index("ctx") * tok_rows + jnp.arange(tok_rows, dtype=jnp.int32)
    block_pair = lax.all_gather(qkv[1:3], "ctx", axis=1, tiled=True)
    key_pos = jnp.arange(block_pair.shape[1], dtype=jnp.int32)
    causal_mask = key_pos[None, :] <= query_pos[:, None]
    out_list = []
    for head_index in range(head_count):
        cols = slice(head_index * HEAD, (head_index + 1) * HEAD)
        scores = (
            lax.dot_general(
                queries[:, cols],
                block_pair[0][:, cols],
                (((1,), (1,)), ((), ())),
                preferred_element_type=jnp.float32,
            )
            * scale
        )
        top = jnp.max(jnp.where(causal_mask, scores, -1e30), axis=1)
        weights = jnp.where(causal_mask, jnp.exp(scores - top[:, None]), 0.0)
        total = jnp.sum(weights, axis=1)
        summed = jnp.dot(
            weights.astype(jnp.bfloat16),
            block_pair[1][:, cols],
            preferred_element_type=jnp.float32,
        )
        out_list.append((summed / total[:, None]).astype(jnp.bfloat16))
    return jnp.concatenate(out_list, 1)


def shards(hyena_in, short_filter, mr_taps, mr_decay, skip, qkv):
    tap_count = mr_taps.shape[1]
    parts = lax.axis_size("ctx")
    scale = 1.0 / math.sqrt(HEAD)
    traded = (qkv.shape[2] // HEAD) % parts == 0
    tail = passed_along(last_rows(hyena_in), "ctx", 1)
    if traded:
        blocks = lax.all_to_all(by_head(qkv, parts), "ctx", 0, 0, tiled=True)
    tap_pos = jnp.arange(tap_count, dtype=jnp.float32)
    filters = mr_taps * jnp.exp(-mr_decay[:, None] * tap_pos[None, :])
    filters_back = jnp.concatenate([filters[:, :1], filters[:, :0:-1]], 1)
    onward, part, gate = hyena_local(hyena_in, tail, short_filter, filters_back, skip[None, :])
    carried = passed_along(onward, "ctx", 1)
    if traded:
        done = head_attention(blocks, scale)
        attn_out = by_token(lax.all_to_all(done, "ctx", 0, 0, tiled=True))
    else:
        attn_out = gathered_attention(qkv, scale)
    carried = jnp.pad(carried.astype(jnp.float32), ((0, REACH), (0, 0)))
    hyena_out = (gate.astype(jnp.float32) * (part + carried)).astype(jnp.bfloat16)
    return (hyena_out, attn_out)


def solution(mesh):
    placed = (
        P(None, ("groups", "ctx"), "tp"),
        P(None, None, "tp"),
        P("tp", None),
        P("tp"),
        P("tp"),
        P(None, ("groups", "ctx"), "tp"),
    )
    return jax.shard_map(
        shards,
        mesh=mesh,
        in_specs=placed,
        out_specs=(P(("groups", "ctx"), "tp"), P(("groups", "ctx"), "tp")),
        check_vma=False,
    )
```

```python
import math

import jax
import jax.numpy as jnp
from jax import lax
from jax.experimental import pallas as pl
from jax.experimental.pallas import tpu as pltpu
from jax.sharding import PartitionSpec as P

HEAD = 128
GW = 16
LANES = 128
EDGE = 8
REACH = 16
ORDER_IN = (0, 3, 2, 6, 7, 5, 4, 1)
ORDER_OUT = (0, 6, 3, 4, 1, 7, 5, 2)


def passed_along(block, axis, distance):
    devices = range(lax.axis_size(axis))
    route = [(i - distance, i) for i in devices if i - distance in devices]
    return lax.ppermute(block, axis, route)


def in_vmem(array):
    return pltpu.with_memory_space_constraint(array, pltpu.VMEM)


ANYWHERE = pl.BlockSpec(memory_space=pl.ANY)


def moved(copies):
    for copy in copies:
        copy.start()
    for copy in copies:
        copy.wait()


def visiting(parts, order):
    return order if len(order) == parts else tuple(range(parts))


def by_head(qkv, order):
    parts = len(order)
    streams, rows, full = qkv.shape
    width = full // parts

    def body(qkv_ref, out_ref, held_ref, sems):
        copies = []
        for p in range(parts):
            held_ref[p] = qkv_ref[:, :, pl.ds(order[p] * width, width)]
            copies.append(pltpu.make_async_copy(held_ref.at[p], out_ref.at[p], sems.at[p]))
            copies[-1].start()
        for copy in copies:
            copy.wait()

    return pl.pallas_call(
        body,
        name="by_head",
        in_specs=[pl.BlockSpec(memory_space=pltpu.VMEM)],
        out_specs=ANYWHERE,
        out_shape=jax.ShapeDtypeStruct((parts, streams, rows, width), qkv.dtype),
        scratch_shapes=[
            pltpu.VMEM((parts, streams, rows, width), qkv.dtype),
            pltpu.SemaphoreType.DMA((parts,)),
        ],
    )(in_vmem(qkv))


def last_rows(x):
    streams, rows, width = x.shape
    tall = REACH + EDGE
    pieces = ((0, tall), (2, tall), (1, EDGE))

    def body(x_ref, out_ref, sems):
        copies = []
        low = 0
        for k, (s, count) in enumerate(pieces):
            copies.append(
                pltpu.make_async_copy(
                    x_ref.at[s, pl.ds(rows - count, count)],
                    out_ref.at[pl.ds(low, count)],
                    sems.at[k],
                )
            )
            low += count
        moved(copies)

    return pl.pallas_call(
        body,
        name="last_rows",
        in_specs=[ANYWHERE],
        out_specs=pl.BlockSpec(memory_space=pltpu.VMEM),
        out_shape=pltpu.VMEM((2 * tall + EDGE, width), x.dtype),
        scratch_shapes=[pltpu.SemaphoreType.DMA((len(pieces),))],
    )(x)


def by_token(blocks, order):
    parts, rows, width = blocks.shape

    def body(in_ref, out_ref, sems):
        moved(
            [
                pltpu.make_async_copy(
                    in_ref.at[p], out_ref.at[:, pl.ds(order[p] * width, width)], sems.at[p]
                )
                for p in range(parts)
            ]
        )

    return pl.pallas_call(
        body,
        name="by_token",
        in_specs=[pl.BlockSpec(memory_space=pltpu.VMEM)],
        out_specs=ANYWHERE,
        out_shape=jax.ShapeDtypeStruct((rows, parts * width), blocks.dtype),
        scratch_shapes=[pltpu.SemaphoreType.DMA((parts,))],
    )(in_vmem(blocks))


def hyena_local(x, tail, short_filter, filters_back, skip):
    streams, rows, width = x.shape
    short_taps = short_filter.shape[1]
    taps = filters_back.shape[1]
    cols = min(512, width)
    per_block = LANES // GW
    tall = REACH + EDGE
    kept = rows - REACH

    def body(x_ref, tail_ref, short_ref, filt_ref, skip_ref, onward_ref, part_ref, gate_ref, *held):
        ext_ref, twice_ref, spread_ref = held
        row = lax.broadcasted_iota(jnp.int32, (rows, taps), 0)
        col = lax.broadcasted_iota(jnp.int32, (rows, taps), 1)
        lane_group = (lax.broadcasted_iota(jnp.int32, (rows, 2 * LANES), 1) % LANES) // GW
        twice_ref[:kept, LANES:] = jnp.zeros((kept, LANES), jnp.bfloat16)
        twice_ref[kept:, :LANES] = jnp.zeros((2 * rows - kept, LANES), jnp.bfloat16)
        for c in range(cols // LANES):
            at = pl.ds(c * LANES, LANES)
            ext_ref[0, c, :tall, :] = tail_ref[:tall, at].astype(jnp.float32)
            ext_ref[2, c, :tall, :] = tail_ref[tall : 2 * tall, at].astype(jnp.float32)
            ext_ref[1, c, REACH:tall, :] = tail_ref[2 * tall :, at].astype(jnp.float32)
            for s in range(streams):
                ext_ref[s, c, tall:, :] = x_ref[s, :, at].astype(jnp.float32)
            out = []
            for s, count in enumerate((REACH + rows, rows, REACH + rows)):
                low = tall + rows - count
                every = count // EDGE
                slabs = [
                    ext_ref[s, c, pl.ds(low + k, EDGE, stride=every), :]
                    for k in range(1 - short_taps, every)
                ]
                heights = [
                    jnp.broadcast_to(short_ref[s, j : j + 1, at], (EDGE, LANES))
                    for j in range(short_taps)
                ]
                sums = []
                for k in range(every):
                    accum = None
                    for j in range(short_taps):
                        piece = heights[j] * slabs[k + short_taps - 1 - j]
                        accum = piece if accum is None else accum + piece
                    sums.append(accum.astype(jnp.bfloat16).astype(jnp.float32))
                out.append(sums)
            for k, (first, last) in enumerate(zip(out[0], out[2])):
                spread_ref[0, c, pl.ds(k, EDGE, stride=len(out[0])), :] = first * last
            for k, middle in enumerate(out[1]):
                spread_ref[1, c, pl.ds(k, EDGE, stride=len(out[1])), :] = middle
            mixed = spread_ref[0, c].astype(jnp.bfloat16)
            gate_ref[:, at] = spread_ref[1, c, :rows].astype(jnp.bfloat16)
            twice_ref[:kept, :LANES] = mixed[REACH : REACH + kept]
            twice_ref[kept:, LANES:] = mixed
            conv = None
            for g in range(per_block):
                base = jnp.broadcast_to(filt_ref[pl.ds(c * per_block + g, 1), :], (rows, taps))
                ring = pltpu.roll(base, 0, 1, stride=1, stride_axis=0)
                band = jnp.concatenate([jnp.where(col > row, ring, 0.0), jnp.where(col <= row, ring, 0.0)], 1).astype(jnp.bfloat16)
                one = jnp.dot(band, twice_ref[...], preferred_element_type=jnp.float32)
                conv = one if g == 0 else jnp.where(lane_group == g, one, conv)
            onward_ref[:, at] = conv[:kept, :LANES].astype(jnp.bfloat16)
            part_ref[:, at] = conv[:, LANES:] + skip_ref[:, at] * mixed[REACH:].astype(jnp.float32)

    wide = pl.BlockSpec((rows, cols), lambda c: (0, c))
    return pl.pallas_call(
        body,
        name="hyena_local",
        grid=(width // cols,),
        in_specs=[
            pl.BlockSpec((streams, rows, cols), lambda c: (0, 0, c)),
            pl.BlockSpec((2 * tall + EDGE, cols), lambda c: (0, c)),
            pl.BlockSpec((streams, short_taps, cols), lambda c: (0, 0, c)),
            pl.BlockSpec((cols // GW, taps), lambda c: (c, 0)),
            pl.BlockSpec((1, cols), lambda c: (0, c)),
        ],
        out_specs=[pl.BlockSpec((kept, cols), lambda c: (0, c)), wide, wide],
        out_shape=[
            jax.ShapeDtypeStruct((kept, width), jnp.bfloat16),
            jax.ShapeDtypeStruct((rows, width), jnp.float32),
            jax.ShapeDtypeStruct((rows, width), jnp.bfloat16),
        ],
        scratch_shapes=[
            pltpu.VMEM((streams, cols // LANES, rows + tall, LANES), jnp.float32),
            pltpu.VMEM((2 * rows, 2 * LANES), jnp.bfloat16),
            pltpu.VMEM((2, cols // LANES, rows + REACH, LANES), jnp.float32),
        ],
        cost_estimate=pl.CostEstimate(
            flops=20 * (width // GW) * LANES * rows * 2 * taps,
            transcendentals=0,
            bytes_accessed=14 * rows * width,
        ),
    )(x, tail, short_filter, filters_back, skip)


def head_attention(blocks, order, order_out, scale):
    parts, _, rows, width = blocks.shape
    step = 2 if parts % 2 == 0 else 1
    q_rows = step * rows
    place = [order.index(token) for token in range(parts)]
    place_out = [order_out.index(token) for token in range(parts)]

    def body(in_ref, out_ref, held_ref, sems):
        copies = []
        row = lax.broadcasted_iota(jnp.int32, (q_rows, q_rows), 0)
        col = lax.broadcasted_iota(jnp.int32, (q_rows, q_rows), 1)
        keep = col <= row

        def stacked(s, at, tokens):
            return jnp.concatenate([in_ref[place[token], s, :, at] for token in tokens], 0)

        for h in range(width // HEAD):
            at = pl.ds(h * HEAD, HEAD)
            for b in reversed(range(parts // step)):
                upto = (b + 1) * step
                query = stacked(0, at, range(b * step, upto))
                keys = stacked(1, at, range(upto))
                values = stacked(2, at, range(upto))
                scores = lax.dot_general(
                    query, keys, (((1,), (1,)), ((), ())), preferred_element_type=jnp.float32
                )
                low = b * q_rows
                edge_scores = jnp.where(keep, scores[:, low:], -1e30)
                if b:
                    scores = jnp.concatenate([scores[:, :low], edge_scores], 1)
                else:
                    scores = edge_scores
                top = jnp.max(scores, axis=1, keepdims=True)
                weights = jnp.exp((scores - top) * scale)
                total = jnp.sum(weights, axis=1, keepdims=True)
                summed = jnp.dot(
                    weights.astype(jnp.bfloat16), values, preferred_element_type=jnp.float32
                )
                done = (summed / total).astype(jnp.bfloat16)
                for k in range(step):
                    token = b * step + k
                    held_ref[place_out[token], :, at] = done[k * rows : (k + 1) * rows]
                    if h == width // HEAD - 1:
                        copies.append(
                            pltpu.make_async_copy(
                                held_ref.at[place_out[token]], out_ref.at[place_out[token]], sems.at[token]
                            )
                        )
                        copies[-1].start()
        for copy in copies:
            copy.wait()

    tokens = parts * rows
    return pl.pallas_call(
        body,
        name="head_attention",
        in_specs=[pl.BlockSpec(memory_space=pltpu.VMEM)],
        out_specs=ANYWHERE,
        scratch_shapes=[
            pltpu.VMEM((parts, rows, width), jnp.bfloat16),
            pltpu.SemaphoreType.DMA((parts,)),
        ],
        out_shape=jax.ShapeDtypeStruct((parts, rows, width), jnp.bfloat16),
        cost_estimate=pl.CostEstimate(
            flops=2 * tokens * tokens * width,
            transcendentals=tokens * tokens * width // (2 * HEAD),
            bytes_accessed=8 * tokens * width,
        ),
    )(in_vmem(blocks))


def gathered_attention(qkv, scale):
    tok_rows = qkv.shape[1]
    head_count = qkv.shape[2] // HEAD
    queries = qkv[0]
    query_pos = lax.axis_index("ctx") * tok_rows + jnp.arange(tok_rows, dtype=jnp.int32)
    block_pair = lax.all_gather(qkv[1:3], "ctx", axis=1, tiled=True)
    key_pos = jnp.arange(block_pair.shape[1], dtype=jnp.int32)
    causal_mask = key_pos[None, :] <= query_pos[:, None]
    out_list = []
    for head_index in range(head_count):
        cols = slice(head_index * HEAD, (head_index + 1) * HEAD)
        scores = (
            lax.dot_general(
                queries[:, cols],
                block_pair[0][:, cols],
                (((1,), (1,)), ((), ())),
                preferred_element_type=jnp.float32,
            )
            * scale
        )
        top = jnp.max(jnp.where(causal_mask, scores, -1e30), axis=1)
        weights = jnp.where(causal_mask, jnp.exp(scores - top[:, None]), 0.0)
        total = jnp.sum(weights, axis=1)
        summed = jnp.dot(
            weights.astype(jnp.bfloat16),
            block_pair[1][:, cols],
            preferred_element_type=jnp.float32,
        )
        out_list.append((summed / total[:, None]).astype(jnp.bfloat16))
    return jnp.concatenate(out_list, 1)


def traded(blocks, order):
    return lax.all_to_all(blocks, "ctx", 0, 0, tiled=True, axis_index_groups=[list(order)])


def shards(hyena_in, short_filter, mr_taps, mr_decay, skip, qkv):
    tap_count = mr_taps.shape[1]
    parts = lax.axis_size("ctx")
    scale = 1.0 / math.sqrt(HEAD)
    whole_heads = (qkv.shape[2] // HEAD) % parts == 0
    tail = passed_along(last_rows(hyena_in), "ctx", 1)
    if whole_heads:
        order, order_out = visiting(parts, ORDER_IN), visiting(parts, ORDER_OUT)
        blocks = traded(by_head(qkv, order), order)
    tap_pos = jnp.arange(tap_count, dtype=jnp.float32)
    filters = mr_taps * jnp.exp(-mr_decay[:, None] * tap_pos[None, :])
    filters_back = jnp.concatenate([filters[:, :1], filters[:, :0:-1]], 1)
    onward, part, gate = hyena_local(hyena_in, tail, short_filter, filters_back, skip[None, :])
    carried = passed_along(onward, "ctx", 1)
    if whole_heads:
        done = head_attention(blocks, order, order_out, scale)
        attn_out = by_token(traded(done, order_out), order_out)
    else:
        attn_out = gathered_attention(qkv, scale)
    carried = jnp.pad(carried.astype(jnp.float32), ((0, REACH), (0, 0)))
    hyena_out = (gate.astype(jnp.float32) * (part + carried)).astype(jnp.bfloat16)
    return (hyena_out, attn_out)


def solution(mesh):
    placed = (
        P(None, ("groups", "ctx"), "tp"),
        P(None, None, "tp"),
        P("tp", None),
        P("tp"),
        P("tp"),
        P(None, ("groups", "ctx"), "tp"),
    )
    return jax.shard_map(
        shards,
        mesh=mesh,
        in_specs=placed,
        out_specs=(P(("groups", "ctx"), "tp"), P(("groups", "ctx"), "tp")),
        check_vma=False,
    )
```

```python
import math

import jax
import jax.numpy as jnp
from jax import lax
from jax.experimental import pallas as pl
from jax.experimental.pallas import tpu as pltpu
from jax.sharding import PartitionSpec as P

HEAD = 128
GW = 16
LANES = 128
EDGE = 8
REACH = 16
ORDER_IN = (0, 6, 3, 4, 1, 7, 5, 2)
ORDER_OUT = (0, 6, 3, 4, 1, 7, 5, 2)


def passed_along(block, axis, distance):
    devices = range(lax.axis_size(axis))
    route = [(i - distance, i) for i in devices if i - distance in devices]
    return lax.ppermute(block, axis, route)


def in_vmem(array):
    return pltpu.with_memory_space_constraint(array, pltpu.VMEM)


ANYWHERE = pl.BlockSpec(memory_space=pl.ANY)


def moved(copies):
    for copy in copies:
        copy.start()
    for copy in copies:
        copy.wait()


def visiting(parts, order):
    return order if len(order) == parts else tuple(range(parts))


def by_head(qkv, order):
    parts = len(order)
    streams, rows, full = qkv.shape
    width = full // parts

    def body(qkv_ref, out_ref, held_ref, sems):
        copies = []
        for p in range(parts):
            held_ref[p] = qkv_ref[:, :, pl.ds(order[p] * width, width)]
            copies.append(pltpu.make_async_copy(held_ref.at[p], out_ref.at[p], sems.at[p]))
            copies[-1].start()
        for copy in copies:
            copy.wait()

    return pl.pallas_call(
        body,
        name="by_head",
        in_specs=[pl.BlockSpec(memory_space=pltpu.VMEM)],
        out_specs=ANYWHERE,
        out_shape=jax.ShapeDtypeStruct((parts, streams, rows, width), qkv.dtype),
        scratch_shapes=[
            pltpu.VMEM((parts, streams, rows, width), qkv.dtype),
            pltpu.SemaphoreType.DMA((parts,)),
        ],
    )(in_vmem(qkv))


def last_rows(x):
    streams, rows, width = x.shape
    tall = REACH + EDGE
    pieces = ((0, tall), (2, tall), (1, EDGE))

    def body(x_ref, out_ref, sems):
        copies = []
        low = 0
        for k, (s, count) in enumerate(pieces):
            copies.append(
                pltpu.make_async_copy(
                    x_ref.at[s, pl.ds(rows - count, count)],
                    out_ref.at[pl.ds(low, count)],
                    sems.at[k],
                )
            )
            low += count
        moved(copies)

    return pl.pallas_call(
        body,
        name="last_rows",
        in_specs=[ANYWHERE],
        out_specs=pl.BlockSpec(memory_space=pltpu.VMEM),
        out_shape=pltpu.VMEM((2 * tall + EDGE, width), x.dtype),
        scratch_shapes=[pltpu.SemaphoreType.DMA((len(pieces),))],
    )(x)


def by_token(blocks, order):
    parts, rows, width = blocks.shape

    def body(in_ref, out_ref, sems):
        moved(
            [
                pltpu.make_async_copy(
                    in_ref.at[p], out_ref.at[:, pl.ds(order[p] * width, width)], sems.at[p]
                )
                for p in range(parts)
            ]
        )

    return pl.pallas_call(
        body,
        name="by_token",
        in_specs=[pl.BlockSpec(memory_space=pltpu.VMEM)],
        out_specs=ANYWHERE,
        out_shape=jax.ShapeDtypeStruct((rows, parts * width), blocks.dtype),
        scratch_shapes=[pltpu.SemaphoreType.DMA((parts,))],
    )(in_vmem(blocks))


def hyena_local(x, tail, short_filter, filters_back, skip):
    streams, rows, width = x.shape
    short_taps = short_filter.shape[1]
    taps = filters_back.shape[1]
    cols = min(512, width)
    per_block = LANES // GW
    tall = REACH + EDGE
    kept = rows - REACH

    def body(x_ref, tail_ref, short_ref, filt_ref, skip_ref, onward_ref, part_ref, gate_ref, *held):
        ext_ref, twice_ref, spread_ref = held
        row = lax.broadcasted_iota(jnp.int32, (rows, taps), 0)
        col = lax.broadcasted_iota(jnp.int32, (rows, taps), 1)
        lane_group = (lax.broadcasted_iota(jnp.int32, (rows, 2 * LANES), 1) % LANES) // GW
        twice_ref[:kept, LANES:] = jnp.zeros((kept, LANES), jnp.bfloat16)
        twice_ref[kept:, :LANES] = jnp.zeros((2 * rows - kept, LANES), jnp.bfloat16)
        for c in range(cols // LANES):
            at = pl.ds(c * LANES, LANES)
            ext_ref[0, c, :tall, :] = tail_ref[:tall, at].astype(jnp.float32)
            ext_ref[2, c, :tall, :] = tail_ref[tall : 2 * tall, at].astype(jnp.float32)
            ext_ref[1, c, REACH:tall, :] = tail_ref[2 * tall :, at].astype(jnp.float32)
            for s in range(streams):
                ext_ref[s, c, tall:, :] = x_ref[s, :, at].astype(jnp.float32)
            out = []
            for s, count in enumerate((REACH + rows, rows, REACH + rows)):
                low = tall + rows - count
                every = count // EDGE
                slabs = [
                    ext_ref[s, c, pl.ds(low + k, EDGE, stride=every), :]
                    for k in range(1 - short_taps, every)
                ]
                heights = [
                    jnp.broadcast_to(short_ref[s, j : j + 1, at], (EDGE, LANES))
                    for j in range(short_taps)
                ]
                sums = []
                for k in range(every):
                    accum = None
                    for j in range(short_taps):
                        piece = heights[j] * slabs[k + short_taps - 1 - j]
                        accum = piece if accum is None else accum + piece
                    sums.append(accum.astype(jnp.bfloat16).astype(jnp.float32))
                out.append(sums)
            for k, (first, last) in enumerate(zip(out[0], out[2])):
                spread_ref[0, c, pl.ds(k, EDGE, stride=len(out[0])), :] = first * last
            for k, middle in enumerate(out[1]):
                spread_ref[1, c, pl.ds(k, EDGE, stride=len(out[1])), :] = middle
            mixed = spread_ref[0, c].astype(jnp.bfloat16)
            gate_ref[:, at] = spread_ref[1, c, :rows].astype(jnp.bfloat16)
            twice_ref[:kept, :LANES] = mixed[REACH : REACH + kept]
            twice_ref[kept:, LANES:] = mixed
            conv = None
            for g in range(per_block):
                base = jnp.broadcast_to(filt_ref[pl.ds(c * per_block + g, 1), :], (rows, taps))
                ring = pltpu.roll(base, 0, 1, stride=1, stride_axis=0)
                band = jnp.concatenate([jnp.where(col > row, ring, 0.0), jnp.where(col <= row, ring, 0.0)], 1).astype(jnp.bfloat16)
                one = jnp.dot(band, twice_ref[...], preferred_element_type=jnp.float32)
                conv = one if g == 0 else jnp.where(lane_group == g, one, conv)
            onward_ref[:, at] = conv[:kept, :LANES].astype(jnp.bfloat16)
            part_ref[:, at] = conv[:, LANES:] + skip_ref[:, at] * mixed[REACH:].astype(jnp.float32)

    wide = pl.BlockSpec((rows, cols), lambda c: (0, c))
    return pl.pallas_call(
        body,
        name="hyena_local",
        grid=(width // cols,),
        in_specs=[
            pl.BlockSpec((streams, rows, cols), lambda c: (0, 0, c)),
            pl.BlockSpec((2 * tall + EDGE, cols), lambda c: (0, c)),
            pl.BlockSpec((streams, short_taps, cols), lambda c: (0, 0, c)),
            pl.BlockSpec((cols // GW, taps), lambda c: (c, 0)),
            pl.BlockSpec((1, cols), lambda c: (0, c)),
        ],
        out_specs=[pl.BlockSpec((kept, cols), lambda c: (0, c)), wide, wide],
        out_shape=[
            jax.ShapeDtypeStruct((kept, width), jnp.bfloat16),
            jax.ShapeDtypeStruct((rows, width), jnp.float32),
            jax.ShapeDtypeStruct((rows, width), jnp.bfloat16),
        ],
        scratch_shapes=[
            pltpu.VMEM((streams, cols // LANES, rows + tall, LANES), jnp.float32),
            pltpu.VMEM((2 * rows, 2 * LANES), jnp.bfloat16),
            pltpu.VMEM((2, cols // LANES, rows + REACH, LANES), jnp.float32),
        ],
        cost_estimate=pl.CostEstimate(
            flops=20 * (width // GW) * LANES * rows * 2 * taps,
            transcendentals=0,
            bytes_accessed=14 * rows * width,
        ),
    )(x, tail, short_filter, filters_back, skip)


def head_attention(blocks, order, order_out, scale):
    parts, _, rows, width = blocks.shape
    step = 2 if parts % 2 == 0 else 1
    q_rows = step * rows
    place = [order.index(token) for token in range(parts)]
    place_out = [order_out.index(token) for token in range(parts)]

    def body(in_ref, out_ref, held_ref, sems):
        copies = []
        row = lax.broadcasted_iota(jnp.int32, (q_rows, q_rows), 0)
        col = lax.broadcasted_iota(jnp.int32, (q_rows, q_rows), 1)
        keep = col <= row

        def stacked(s, at, tokens):
            return jnp.concatenate([in_ref[place[token], s, :, at] for token in tokens], 0)

        for h in range(width // HEAD):
            at = pl.ds(h * HEAD, HEAD)
            spans = list(reversed(range(parts // step)))

            def scored(b):
                upto = (b + 1) * step
                scores = lax.dot_general(
                    stacked(0, at, range(b * step, upto)),
                    stacked(1, at, range(upto)),
                    (((1,), (1,)), ((), ())),
                    preferred_element_type=jnp.float32,
                )
                low = b * q_rows
                edge_scores = jnp.where(keep, scores[:, low:], -1e30)
                if b:
                    return jnp.concatenate([scores[:, :low], edge_scores], 1)
                return edge_scores

            def weighed(scores):
                top = jnp.max(scores, axis=1, keepdims=True)
                weights = jnp.exp((scores - top) * scale)
                return weights.astype(jnp.bfloat16), jnp.sum(weights, axis=1, keepdims=True)

            def finished(b, weights, total):
                values = stacked(2, at, range((b + 1) * step))
                summed = jnp.dot(weights, values, preferred_element_type=jnp.float32)
                done = (summed / total).astype(jnp.bfloat16)
                for k in range(step):
                    token = b * step + k
                    held_ref[place_out[token], :, at] = done[k * rows : (k + 1) * rows]
                    if h == width // HEAD - 1:
                        copies.append(
                            pltpu.make_async_copy(
                                held_ref.at[place_out[token]],
                                out_ref.at[place_out[token]],
                                sems.at[token],
                            )
                        )
                        copies[-1].start()

            ahead = scored(spans[0])
            for k, b in enumerate(spans):
                scores = ahead
                if k + 1 < len(spans):
                    ahead = scored(spans[k + 1])
                finished(b, *weighed(scores))
        for copy in copies:
            copy.wait()

    tokens = parts * rows
    return pl.pallas_call(
        body,
        name="head_attention",
        in_specs=[pl.BlockSpec(memory_space=pltpu.VMEM)],
        out_specs=ANYWHERE,
        scratch_shapes=[
            pltpu.VMEM((parts, rows, width), jnp.bfloat16),
            pltpu.SemaphoreType.DMA((parts,)),
        ],
        out_shape=jax.ShapeDtypeStruct((parts, rows, width), jnp.bfloat16),
        cost_estimate=pl.CostEstimate(
            flops=2 * tokens * tokens * width,
            transcendentals=tokens * tokens * width // (2 * HEAD),
            bytes_accessed=8 * tokens * width,
        ),
    )(in_vmem(blocks))


def gathered_attention(qkv, scale):
    tok_rows = qkv.shape[1]
    head_count = qkv.shape[2] // HEAD
    queries = qkv[0]
    query_pos = lax.axis_index("ctx") * tok_rows + jnp.arange(tok_rows, dtype=jnp.int32)
    block_pair = lax.all_gather(qkv[1:3], "ctx", axis=1, tiled=True)
    key_pos = jnp.arange(block_pair.shape[1], dtype=jnp.int32)
    causal_mask = key_pos[None, :] <= query_pos[:, None]
    out_list = []
    for head_index in range(head_count):
        cols = slice(head_index * HEAD, (head_index + 1) * HEAD)
        scores = (
            lax.dot_general(
                queries[:, cols],
                block_pair[0][:, cols],
                (((1,), (1,)), ((), ())),
                preferred_element_type=jnp.float32,
            )
            * scale
        )
        top = jnp.max(jnp.where(causal_mask, scores, -1e30), axis=1)
        weights = jnp.where(causal_mask, jnp.exp(scores - top[:, None]), 0.0)
        total = jnp.sum(weights, axis=1)
        summed = jnp.dot(
            weights.astype(jnp.bfloat16),
            block_pair[1][:, cols],
            preferred_element_type=jnp.float32,
        )
        out_list.append((summed / total[:, None]).astype(jnp.bfloat16))
    return jnp.concatenate(out_list, 1)


def traded(blocks, order):
    return lax.all_to_all(blocks, "ctx", 0, 0, tiled=True, axis_index_groups=[list(order)])


def shards(hyena_in, short_filter, mr_taps, mr_decay, skip, qkv):
    tap_count = mr_taps.shape[1]
    parts = lax.axis_size("ctx")
    scale = 1.0 / math.sqrt(HEAD)
    whole_heads = (qkv.shape[2] // HEAD) % parts == 0
    tail = passed_along(last_rows(hyena_in), "ctx", 1)
    if whole_heads:
        order, order_out = visiting(parts, ORDER_IN), visiting(parts, ORDER_OUT)
        blocks = traded(by_head(qkv, order), order)
    tap_pos = jnp.arange(tap_count, dtype=jnp.float32)
    filters = mr_taps * jnp.exp(-mr_decay[:, None] * tap_pos[None, :])
    filters_back = jnp.concatenate([filters[:, :1], filters[:, :0:-1]], 1)
    onward, part, gate = hyena_local(hyena_in, tail, short_filter, filters_back, skip[None, :])
    carried = passed_along(onward, "ctx", 1)
    if whole_heads:
        done = head_attention(blocks, order, order_out, scale)
        attn_out = by_token(traded(done, order_out), order_out)
    else:
        attn_out = gathered_attention(qkv, scale)
    carried = jnp.pad(carried.astype(jnp.float32), ((0, REACH), (0, 0)))
    hyena_out = (gate.astype(jnp.float32) * (part + carried)).astype(jnp.bfloat16)
    return (hyena_out, attn_out)


def solution(mesh):
    placed = (
        P(None, ("groups", "ctx"), "tp"),
        P(None, None, "tp"),
        P("tp", None),
        P("tp"),
        P("tp"),
        P(None, ("groups", "ctx"), "tp"),
    )
    return jax.shard_map(
        shards,
        mesh=mesh,
        in_specs=placed,
        out_specs=(P(("groups", "ctx"), "tp"), P(("groups", "ctx"), "tp")),
        check_vma=False,
    )
```
